256 devices in a mesh: frame: 32 (over z_lo, y, core), mod: 2 (over z_hi), row: 4 (over x).
Axes of the slice: x: 4, y: 4, z: 8 (z_hi: 2, z_lo: 4; z = z_hi * 4 + z_lo), core: 2. Of those that a mesh axis runs over, the one named last changes fastest.
Arguments:
- amplitude: float32 [512, 512], P('row'), may hold values from 0.25 to 1.75
- pupil_mask: int32 [512, 512], P('row'), may hold values 0 or 1
- phase_common: float32 [512, 512], P('row'), may hold values from -3 to 3
- screens: float32 [32, 512, 512], P('frame', 'row'), may hold values from -6 to 6
- offsets: int32 [2, 2], P('mod'), may hold values from -8 to 8
- measured: float32 [32, 1024, 1024], P('frame', 'row'), may hold values from 0 to 0.5
- valid: int32 [1024, 1024], P('row'), may hold values 0 or 1
Outputs:
- intensity: float32 [32, 1024, 1024], P('frame', 'row', 'mod')
- phase_grad: float32 [512, 512], P('row')
- amp_grad: float32 [512, 512], P('row')
The draws below stay inside these ranges and needn't reach their ends.
All inputs are finite; a program needn't handle non-finite values. No bound on the sum of `pupil_mask` or of `valid` on one device may be relied on, other than what follows from the above.
Results may differ from the reference program's by a relative error of at most 0.017.
Values may be sent and summed in bfloat16 or wider, within the bound.
No kernel may reach another device: no remote copies, remote signals or barrier semaphores. Data moves between devices by JAX's collectives and lax.ppermute only.
A program may use at most 64 MiB of HBM per device.

```python
import math
import jax
import jax.numpy as jnp
from jax import lax

PUPIL = 512
PADDED = 1024
MOD_DEV = 1
MODS = 2
FRAMES = 32
N_MOD = 2


def place_ends(drawn, rng, low, high):
    shape = drawn.shape
    spot = [jax.random.randint(jax.random.fold_in(rng, axis), (), 0, shape[axis]) for axis in range(len(shape))]
    drawn = drawn.at[tuple(spot)].set(low)
    longest = shape.index(max(shape))
    spot[longest] = (spot[longest] + 1) % shape[longest]
    return drawn.at[tuple(spot)].set(high)


def level_of(rng, shape, shards, low, largest):
    def one(axis_at, blocks):
        steps = jax.random.uniform(jax.random.fold_in(jax.random.fold_in(rng, 6), axis_at), (blocks,), jnp.float32, low / len(shards), largest / len(shards))
        return jnp.repeat(jnp.exp(steps), shape[axis_at] // blocks).reshape((-1,) + (1,) * (len(shape) - axis_at - 1))

    level = one(*shards[0])
    for cut in shards[1:]:
        level = level * one(*cut)
    return level


def scatter_about(own_key, extent, deviation, most, pieces=(), held_as=jnp.bfloat16):
    array = jax.random.normal(own_key, extent, jnp.float32) * deviation
    if len(pieces) > 0:
        array = level_of(own_key, extent, pieces, -0.22, 0.18) * array
    return jnp.clip(array, min=-most, max=most).astype(held_as)


def setup_inputs(seed: int = 0) -> dict:
    keys = jax.random.split(jax.random.key(seed), 8)
    return {
        "amplitude": jnp.clip(1.0 + 0.15 * jax.random.normal(keys[0], (PUPIL, PUPIL), jnp.float32), 0.25, 1.75),
        "pupil_mask": place_ends((jax.random.randint(keys[1], (PUPIL, PUPIL), 0, 8) < 7).astype(jnp.int32), jax.random.fold_in(keys[1], 1), 0, 1),
        "phase_common": scatter_about(keys[2], (PUPIL, PUPIL), 0.5, 3.0, ((0, 4),), jnp.float32),
        "screens": scatter_about(keys[3], (FRAMES, PUPIL, PUPIL), 1.0, 6.0, ((0, 32), (1, 4)), jnp.float32),
        "offsets": place_ends(jax.random.randint(keys[4], (MODS, 2), -8, 9), jax.random.fold_in(keys[4], 1), -8, 8).astype(jnp.int32),
        "measured": jnp.clip(0.5 * jax.random.uniform(keys[5], (FRAMES, PADDED, PADDED), jnp.float32) ** level_of(keys[5], (FRAMES, PADDED, PADDED), ((0, 32), (1, 4)), -0.2, 0.2), 0.0, 0.5),
        "valid": place_ends((jax.random.randint(keys[6], (PADDED, PADDED), 0, 4) < 3).astype(jnp.int32), jax.random.fold_in(keys[6], 1), 0, 1),
    }


def twiddle(row_index, col_index, period, direction):
    product = (row_index[:, None] * col_index[None, :]) % period
    angles = (direction * 2.0 * math.pi / period) * product.astype(jnp.float32)
    return jnp.cos(angles), jnp.sin(angles)


def pyramid(row_index, col_index, offset_pair, pupil_width, full_width):
    spread = jnp.abs(row_index - offset_pair[0])[:, None] + jnp.abs(col_index - offset_pair[1])[None, :]
    angles = (math.pi / full_width) * ((pupil_width * spread) % (2 * full_width)).astype(jnp.float32)
    return jnp.cos(angles), jnp.sin(angles)


def to_bfloat(complex_pair):
    return complex_pair[0].astype(jnp.bfloat16), complex_pair[1].astype(jnp.bfloat16)


def conjugate(complex_pair):
    return complex_pair[0], -complex_pair[1]


def complex_dot(left_pair, right_pair):
    real_part = jnp.dot(left_pair[0], right_pair[0], preferred_element_type=jnp.float32) - jnp.dot(left_pair[1], right_pair[1], preferred_element_type=jnp.float32)
    imag_part = jnp.dot(left_pair[0], right_pair[1], preferred_element_type=jnp.float32) + jnp.dot(left_pair[1], right_pair[0], preferred_element_type=jnp.float32)
    return real_part, imag_part


def modulate(focal_field, face_mask):
    return to_bfloat((focal_field[0] * face_mask[0] - focal_field[1] * face_mask[1], focal_field[0] * face_mask[1] + focal_field[1] * face_mask[0]))


def demodulate(back_pass, face_mask):
    return face_mask[0] * back_pass[0] + face_mask[1] * back_pass[1], face_mask[0] * back_pass[1] - face_mask[1] * back_pass[0]


def reference(amplitude, pupil_mask, phase_common, screens, offsets, measured, valid):
    pupil_idx = jnp.arange(PUPIL, dtype=jnp.int32) - PUPIL // 2
    focal_idx = jnp.arange(PADDED, dtype=jnp.int32) - PADDED // 2
    w_tab = to_bfloat(twiddle(pupil_idx, focal_idx, PADDED, -1.0))
    wt_tab = to_bfloat(twiddle(focal_idx, pupil_idx, PADDED, -1.0))
    g_raw = twiddle(focal_idx, focal_idx, PADDED, 1.0)
    g_tab = to_bfloat((g_raw[0] / PADDED, g_raw[1] / PADDED))
    g_conj = conjugate(g_tab)
    w_conj = conjugate(w_tab)
    wt_conj = conjugate(wt_tab)
    mask_float = pupil_mask.astype(jnp.float32)
    weight = amplitude * mask_float
    live_pixels = valid.astype(jnp.float32)
    adjoint_scale = 2.0 / MODS
    grouped_offsets = offsets.reshape(N_MOD, MOD_DEV, 2)

    def one_frame(scan_items):
        screen, target = scan_items
        phase_total = phase_common + screen
        cosine = jnp.cos(phase_total)
        sine_part = jnp.sin(phase_total)
        pupil_field = (weight * cosine, weight * sine_part)
        first_pass = to_bfloat(complex_dot(to_bfloat(pupil_field), w_tab))
        focal_field = to_bfloat(complex_dot(wt_tab, first_pass))

        def forward(running, offset_pair):
            face_mask = pyramid(focal_idx, focal_idx, offset_pair, PUPIL, PADDED)
            inner_pass = to_bfloat(complex_dot(g_tab, modulate(focal_field, face_mask)))
            detector = complex_dot(inner_pass, g_tab)
            return running + detector[0] * detector[0] + detector[1] * detector[1], detector

        running, detectors = lax.scan(forward, jnp.zeros((PADDED, PADDED), jnp.float32), offsets)
        intensity = running / MODS
        residual = live_pixels * (intensity - target)

        def adjoint(running_pair, scan_parts):
            offset_pair, det_real, det_imag = scan_parts
            face_mask = pyramid(focal_idx, focal_idx, offset_pair, PUPIL, PADDED)
            weighted = to_bfloat((adjoint_scale * residual * det_real, adjoint_scale * residual * det_imag))
            inner_pass = to_bfloat(complex_dot(weighted, g_conj))
            back_pass = demodulate(complex_dot(g_conj, inner_pass), face_mask)
            return (running_pair[0] + back_pass[0], running_pair[1] + back_pass[1]), None

        def group(pupil_pair, group_items):
            group_offsets, group_real, group_imag = group_items
            zero_focal = jnp.zeros((PADDED, PADDED), jnp.float32)
            group_sum, _ = lax.scan(adjoint, (zero_focal, zero_focal), (group_offsets, group_real, group_imag))
            spread_back = to_bfloat(complex_dot(w_conj, to_bfloat(group_sum)))
            pupil_back = complex_dot(spread_back, wt_conj)
            return (pupil_pair[0] + pupil_back[0], pupil_pair[1] + pupil_back[1]), None

        zero_pupil = jnp.zeros((PUPIL, PUPIL), jnp.float32)
        group_real = detectors[0].reshape(N_MOD, MOD_DEV, PADDED, PADDED)
        group_imag = detectors[1].reshape(N_MOD, MOD_DEV, PADDED, PADDED)
        pupil_back, _ = lax.scan(group, (zero_pupil, zero_pupil), (grouped_offsets, group_real, group_imag))
        phase_term = pupil_back[1] * pupil_field[0] - pupil_back[0] * pupil_field[1]
        amp_term = mask_float * (pupil_back[0] * cosine + pupil_back[1] * sine_part)
        return intensity, phase_term, amp_term

    intensity, phase_terms, amp_terms = lax.map(one_frame, (screens, measured))
    phase_grad = jnp.sum(phase_terms, axis=0) / FRAMES
    amp_grad = jnp.sum(amp_terms, axis=0) / FRAMES
    return intensity, phase_grad, amp_grad
```

```python
import functools
import math

import jax
import jax.numpy as jnp
from jax import lax
from jax.experimental import pallas as pl
from jax.experimental.pallas import tpu as pltpu
from jax.sharding import Mesh
from jax.sharding import PartitionSpec as P

BF = jnp.bfloat16
F32 = jnp.float32
PUPIL = 512
FULL = 1024
ROWS = 256
COLS = 512
BLOCK = 128
VMEM = pltpu.VMEM
SMEM = pltpu.SMEM


def sincos(angle):
    turns = jnp.floor(angle * (2.0 / math.pi) + 0.5)
    rest = angle - turns * 1.5703125
    rest = rest - turns * 4.837512969970703125e-4
    rest = rest - turns * 7.549789954891882e-8
    quadrant = turns.astype(jnp.int32)
    square = rest * rest
    sine = rest + rest * square * (
        -1.6666654611e-1 + square * (8.3321608736e-3 + square * -1.9515295891e-4)
    )
    cosine = (
        1.0
        - 0.5 * square
        + square
        * square
        * (4.166664568298827e-2 + square * (-1.388731625493765e-3 + square * 2.443315711809948e-5))
    )
    odd = (quadrant & 1) == 1
    sin_out = jnp.where(odd, cosine, sine)
    cos_out = jnp.where(odd, sine, cosine)
    sin_out = jnp.where((quadrant & 2) != 0, -sin_out, sin_out)
    cos_out = jnp.where(((quadrant + 1) & 2) != 0, -cos_out, cos_out)
    return sin_out, cos_out


def unit_sincos(steps):
    return sincos((steps & (2 * FULL - 1)).astype(F32) * (math.pi / FULL))


def dot(left, right):
    return jnp.dot(left, right, preferred_element_type=F32)


def dot_t(left, right):
    return lax.dot_general(left, right, (((1,), (1,)), ((), ())), preferred_element_type=F32)


def response(lag, offset):
    count_up = FULL // 2 - offset
    count_down = FULL // 2 + offset
    step_up = (lag + FULL // 4) & (FULL - 1)
    step_down = (FULL // 4 - lag) & (FULL - 1)
    shift = 2 * lag * offset

    def ratio(step, count):
        over, _ = unit_sincos(step * count)
        under, _ = unit_sincos(step)
        flat = step == 0
        return jnp.where(flat, count.astype(F32), over / jnp.where(flat, 1.0, under))

    size_up = ratio(step_up, count_up) * (1.0 / FULL)
    size_down = ratio(step_down, count_down) * (1.0 / FULL)
    sin_up, cos_up = unit_sincos((count_up - 1) * step_up + shift)
    sin_down, cos_down = unit_sincos((count_down + 1) * step_down + shift)
    return size_up * cos_up + size_down * cos_down, size_up * sin_up + size_down * sin_down


def field_kernel(amp_ref, mask_ref, phase_ref, screen_ref, out_ref):
    sine, cosine = sincos(phase_ref[...] + screen_ref[...])
    weight = amp_ref[...] * mask_ref[...].astype(F32)
    out_ref[:, :PUPIL] = (weight * cosine).astype(BF)
    out_ref[:, PUPIL:] = (weight * sine).astype(BF)


def table_kernel(place_ref, offset_ref, left_ref, back_ref, right_ref, strip_ref):
    row_at = place_ref[0]
    mod_at = place_ref[1]
    lane = lax.broadcasted_iota(jnp.int32, (8, FULL), 1)

    def strips(parts):
        for part in range(2):
            base = pltpu.roll(parts[part], 0, 1, stride=1, stride_axis=0)
            for group in range(0, BLOCK, 16):
                low = pltpu.roll(base, group, 1) if group else base
                high = pltpu.roll(base, group + 8, 1)
                strip_ref[part, pl.ds(group, 16), :] = jnp.concatenate([low, high], axis=0).astype(BF)

    def window(part, blocks):
        start = pl.multiple_of((blocks & 7) * BLOCK, BLOCK)
        return strip_ref[part, :, pl.ds(start, BLOCK)]

    def each(count):
        return [(part, i, k) for part in range(2) for i in range(count[0]) for k in range(count[1])]

    row_offset = offset_ref[0, 0]
    strips(response(-lane - FULL // 4, row_offset))
    for part, i, d in each((ROWS // BLOCK, 4)):
        left_ref[part, pl.ds(i * BLOCK, BLOCK), pl.ds(d * BLOCK, BLOCK)] = window(
            part, ((row_at + d) & 3) - 2 * row_at - i
        )
    strips(response(lane - FULL // 4, row_offset))
    for part, d, i in each((4, ROWS // BLOCK)):
        back_ref[part, pl.ds(d * BLOCK, BLOCK), pl.ds(i * BLOCK, BLOCK)] = window(
            part, 2 * row_at + i - ((row_at + d) & 3)
        )
    strips(response(-lane - FULL // 4, offset_ref[0, 1]))
    for part, i, k in each((4, 4)):
        right_ref[part, pl.ds(i * BLOCK, BLOCK), pl.ds(k * BLOCK, BLOCK)] = window(
            part, k - 4 * mod_at - i
        )


def detector_kernel(
    left_a, left_b, right_a, right_b, e0, e1, e2, e3, measured_ref, valid_ref, image_ref, back_ref,
    pupil_ref, half_ref, det_ref, weighted_ref,
):
    for d, block in enumerate((e0, e1, e2, e3)):
        pupil_ref[pl.ds(d * BLOCK, BLOCK), :] = block[...]
    lefts, rights = (left_a, left_b), (right_a, right_b)
    wide = 256
    for m in range(2):
        for at in range(0, PUPIL, wide):
            real = pupil_ref[:, pl.ds(at, wide)]
            imag = pupil_ref[:, pl.ds(PUPIL + at, wide)]
            half_ref[m, :, pl.ds(at, wide)] = (
                dot(lefts[m][0], real) - dot(lefts[m][1], imag)
            ).astype(BF)
            half_ref[m, :, pl.ds(PUPIL + at, wide)] = (
                dot(lefts[m][0], imag) + dot(lefts[m][1], real)
            ).astype(BF)
    for at in range(0, COLS, wide):
        total = None
        for m in range(2):
            real = rights[m][0, pl.ds(at, wide), :]
            imag = rights[m][1, pl.ds(at, wide), :]
            half_real = half_ref[m, :, :PUPIL]
            half_imag = half_ref[m, :, PUPIL:]
            det_real = dot_t(half_real, real) - dot_t(half_imag, imag)
            det_imag = dot_t(half_real, imag) + dot_t(half_imag, real)
            det_ref[m, 0] = det_real
            det_ref[m, 1] = det_imag
            power = det_real * det_real + det_imag * det_imag
            total = power if total is None else total + power
        image = 0.5 * total
        image_ref[:, pl.ds(at, wide)] = image
        residual = valid_ref[:, pl.ds(at, wide)].astype(F32) * (
            image - measured_ref[:, pl.ds(at, wide)]
        )
        for m in range(2):
            for part in range(2):
                weighted_ref[m, part, :, pl.ds(at, wide)] = (residual * det_ref[m, part]).astype(BF)
    for m in range(2):
        real_in = weighted_ref[m, 0]
        imag_in = weighted_ref[m, 1]
        for at in range(0, PUPIL, wide):
            real = rights[m][0, :, pl.ds(at, wide)]
            imag = rights[m][1, :, pl.ds(at, wide)]
            back_ref[m, :, pl.ds(at, wide)] = (dot(real_in, real) + dot(imag_in, imag)).astype(BF)
            back_ref[m, :, pl.ds(PUPIL + at, wide)] = (
                dot(imag_in, real) - dot(real_in, imag)
            ).astype(BF)


def gradient_kernel(d, back_a, back_b, half_ref, pupil_ref, out_ref):
    backs = (back_a, back_b)
    wide = 256
    here = pl.ds(d * BLOCK, BLOCK)
    for at in range(0, PUPIL, wide):
        real = imag = None
        for m in range(2):
            half_real = half_ref[m, :, pl.ds(at, wide)]
            half_imag = half_ref[m, :, pl.ds(PUPIL + at, wide)]
            table_real = backs[m][0, here, :]
            table_imag = backs[m][1, here, :]
            more_real = dot(table_real, half_real) + dot(table_imag, half_imag)
            more_imag = dot(table_real, half_imag) - dot(table_imag, half_real)
            real = more_real if real is None else real + more_real
            imag = more_imag if imag is None else imag + more_imag
        field_real = pupil_ref[:, pl.ds(at, wide)].astype(F32)
        field_imag = pupil_ref[:, pl.ds(PUPIL + at, wide)].astype(F32)
        out_ref[:, pl.ds(at, wide)] = (real * field_real + imag * field_imag).astype(BF)
        out_ref[:, pl.ds(PUPIL + at, wide)] = (imag * field_real - real * field_imag).astype(BF)


TILE = 16
PIECES = BLOCK * PUPIL // (TILE * 128)


def fold_kernel(core_ref, s0, s1, s2, s3, keep_ref, send_ref):
    first = core_ref[0] == 0
    for k in range(4):
        for r in range(BLOCK // TILE):
            rows = pl.ds(r * TILE, TILE)
            sums = []
            for part in range(2):
                at = pl.ds(part * PUPIL + k * 128, 128)
                sums.append(
                    s0[rows, at].astype(F32)
                    + s1[rows, at].astype(F32)
                    + s2[rows, at].astype(F32)
                    + s3[rows, at].astype(F32)
                )
            piece = k * (BLOCK // TILE) + r
            keep_ref[piece] = jnp.where(first, sums[0], sums[1]).astype(BF)
            send_ref[piece] = jnp.where(first, sums[1], sums[0]).astype(BF)


def spread_kernel(got_ref, out_ref):
    total = jnp.sum(got_ref[...].astype(F32), axis=0).astype(BF)
    out_ref[...] = jnp.broadcast_to(total[None], out_ref.shape)


def finish_kernel(frames, core_ref, own_ref, other_ref, amp_ref, phase_out, amp_out):
    first = core_ref[0] == 0
    for k in range(4):
        for r in range(BLOCK // TILE):
            rows, at = pl.ds(r * TILE, TILE), pl.ds(k * 128, 128)
            piece = k * (BLOCK // TILE) + r
            own = own_ref[piece].astype(F32)
            other = other_ref[piece].astype(F32)
            amp_out[rows, at] = jnp.where(first, own, other) / (frames * amp_ref[rows, at])
            phase_out[rows, at] = jnp.where(first, other, own) * (1.0 / frames)


def struct(shape, dtype):
    return jax.ShapeDtypeStruct(shape, dtype)


def call(kernel, outs, scalars, vectors, scratch=(), flops=0):
    specs = [pl.BlockSpec(memory_space=SMEM)] * len(scalars) + [
        pl.BlockSpec(memory_space=VMEM)
    ] * len(vectors)
    moved = sum(math.prod(v.shape) * v.dtype.itemsize for v in vectors)
    return pl.pallas_call(
        kernel,
        out_shape=outs,
        in_specs=specs,
        out_specs=jax.tree.map(lambda _: pl.BlockSpec(memory_space=VMEM), outs),
        scratch_shapes=list(scratch),
        cost_estimate=pl.CostEstimate(flops=flops, bytes_accessed=moved, transcendentals=0),
    )(*scalars, *vectors)


def tables(place, offset_pair):
    return call(
        table_kernel,
        [
            struct((2, ROWS, PUPIL), BF),
            struct((2, PUPIL, ROWS), BF),
            struct((2, COLS, PUPIL), BF),
        ],
        (place, offset_pair),
        (),
        [VMEM((2, BLOCK, FULL), BF)],
        flops=4_000_000,
    )


def detector(left_a, left_b, right_a, right_b, fields, target, live):
    return call(
        detector_kernel,
        [struct((ROWS, COLS), F32), struct((2, ROWS, 2 * PUPIL), BF)],
        (),
        (left_a, left_b, right_a, right_b, *fields, target, live),
        [
            VMEM((PUPIL, 2 * PUPIL), BF),
            VMEM((2, ROWS, 2 * PUPIL), BF),
            VMEM((2, 2, ROWS, 256), F32),
            VMEM((2, 2, ROWS, COLS), BF),
        ],
        flops=3_221_000_000,
    )


def gradient(d, back_a, back_b, half, field):
    return call(
        functools.partial(gradient_kernel, d),
        struct((BLOCK, 2 * PUPIL), BF),
        (),
        (back_a, back_b, half, field),
        flops=268_000_000,
    )


def shards(amplitude, pupil_mask, phase_common, screens, offsets, measured, valid):
    row_at = lax.axis_index("x")
    mod_at = lax.axis_index("zh")
    core = lax.axis_index("core").astype(jnp.int32).reshape(1)
    place = jnp.stack([row_at, mod_at]).astype(jnp.int32)
    ring = lambda d: [(i, (i + d) % 4) for i in range(4)]
    swap = [(0, 1), (1, 0)]
    frames = 32

    field = call(
        field_kernel,
        struct((BLOCK, 2 * PUPIL), BF),
        (),
        (amplitude, pupil_mask, phase_common, screens[0]),
    )
    fields = [field] + [lax.ppermute(field, "x", ring(-d)) for d in (1, 2, 3)]
    offsets_b = lax.ppermute(offsets, "zh", swap)
    left_a, back_a, right_a = tables(place, offsets)
    left_b, back_b, right_b = tables(place, offsets_b)
    target = lax.dynamic_slice_in_dim(measured[0], mod_at * COLS, COLS, 1)
    live = lax.dynamic_slice_in_dim(valid, mod_at * COLS, COLS, 1)
    image, half = detector(left_a, left_b, right_a, right_b, fields, target, live)
    arrived = []
    for d in (2, 1, 3):
        part = gradient(d, back_a, back_b, half, fields[d])
        arrived.append(lax.ppermute(part, "x", ring(d)))
    own = gradient(0, back_a, back_b, half, fields[0])
    keep, send = call(
        fold_kernel, [struct((PIECES, TILE, 128), BF)] * 2, (core,), (own, *arrived)
    )
    keep = (keep.astype(F32) + lax.ppermute(send, "core", swap).astype(F32)).astype(BF)
    around = ("y", "zh", "zl")
    got = lax.all_to_all(keep, around, 0, 0)
    spread = call(spread_kernel, struct((PIECES, TILE, 128), BF), (), (got,))
    mine = lax.all_to_all(spread, around, 0, 0)
    other = lax.ppermute(mine, "core", swap)
    phase_grad, amp_grad = call(
        functools.partial(finish_kernel, frames),
        [struct((BLOCK, PUPIL), F32)] * 2,
        (core,),
        (mine, other, amplitude),
    )
    return image[None], phase_grad, amp_grad


def solution(mesh):
    fine = Mesh(mesh.devices.reshape(4, 4, 2, 2, 4), ("zl", "y", "core", "zh", "x"))
    frame = ("zl", "y", "core")
    rows = P("x", None)
    return jax.shard_map(
        shards,
        mesh=fine,
        in_specs=(
            rows, rows, rows, P(frame, "x", None), P("zh", None), P(frame, "x", None), rows
        ),
        out_specs=(P(frame, "x", "zh"), rows, rows),
        check_vma=False,
    )
```
